32 devices in a mesh: dp: 16 (over z, x, core), mp: 2 (over y).
Axes of the slice: x: 2, y: 2, z: 4, core: 2. Of those that a mesh axis runs over, the one named last changes fastest.
Arguments:
- tokens: bfloat16 [64, 256, 1152], P('dp'), may hold values from -6 to 6
- conditioning: bfloat16 [64, 1152], P('dp'), may hold values from -6 to 6
- bucket_ids: int32 [64], P('dp'), may hold values from 0 to 2, as said below
- keep_order: int32 [64, 128], P('dp'), may hold values from 0 to 255, as said below
- group_counts: int32 [16], P('dp'), may hold values from 1 to 4, as said below
- cotangent: bfloat16 [64, 256, 1152], P('dp'), may hold values from -6 to 6
- modulation_weight: bfloat16 [1152, 6912], P('dp'), may hold values from -0.1875 to 0.1875
- modulation_bias: bfloat16 [6912], replicated, may hold values from -3 to 3
- input_weight: bfloat16 [3, 1152, 1152], P(None, 'dp', 'mp'), may hold values from -0.1875 to 0.1875
- query_value_bias: bfloat16 [2, 1152], P(None, 'mp'), may hold values from -3 to 3
- output_weight: bfloat16 [1152, 1152], P('mp', 'dp'), may hold values from -0.75 to 0.75
- output_bias: bfloat16 [1152], replicated, may hold values from -2 to 2
- expand_weight: bfloat16 [1152, 4608], P('dp', 'mp'), may hold values from -0.1875 to 0.1875
- expand_bias: bfloat16 [4608], P('mp'), may hold values from -3 to 3
- shrink_weight: bfloat16 [4608, 1152], P('mp', 'dp'), may hold values from -0.09375 to 0.09375
- shrink_bias: bfloat16 [1152], replicated, may hold values from -2 to 2
Outputs:
- block_out: bfloat16 [64, 256, 1152], P('dp')
- tokens_grad: bfloat16 [64, 256, 1152], P('dp')
- modulation_weight_grad: float32 [1152, 6912], P('dp')
- modulation_bias_grad: float32 [6912], replicated
- input_weight_grad: float32 [3, 1152, 1152], P(None, 'dp', 'mp')
- query_value_bias_grad: float32 [2, 1152], P(None, 'mp')
- output_weight_grad: float32 [1152, 1152], P('mp', 'dp')
- output_bias_grad: float32 [1152], replicated
- expand_weight_grad: float32 [1152, 4608], P('dp', 'mp')
- expand_bias_grad: float32 [4608], P('mp')
- shrink_weight_grad: float32 [4608, 1152], P('mp', 'dp')
- shrink_bias_grad: float32 [1152], replicated
The draws below stay inside these ranges and needn't reach their ends.
Inputs may be any that keep to these rules, and one draw needn't show every extreme that they name: `bucket_ids`: buckets 0, 1 and 2 stand for grids of 16 x 16, 12 x 20 and 20 x 12 patches. `keep_order`: row i holds 128 distinct slot numbers; its first valid-length entries (half of image i's length) are real token slots of that image chosen at random, the remaining entries are other slots of that image. Group g holds live images in its first group_counts[g] of 4 image slots; in every draw some group is full.
All inputs are finite; a program needn't handle non-finite values.
Results may differ from the reference program's by a relative error of at most 0.015.
The reference program's roundings to bfloat16 on the way count: a program that leaves them out, or rounds other values in their place, can miss the bound.
Values may be sent and summed in bfloat16 or wider, within the bound.
A program may use at most 144 MiB of HBM per device.

```python
import jax
import jax.numpy as jnp
from jax import lax

D = 1152
HEADS = 16
HEAD_DIM = 72
FF = 4608
SLOTS = 256
KEEP = 128
IMG_MB = 2
MICRO = 2
IMAGES = 64


def routing_tables(key):
    buckets = jax.random.randint(jax.random.fold_in(key, 11), (IMAGES,), 0, 3).astype(jnp.int32)
    lengths = jnp.where(buckets == 0, SLOTS, SLOTS - SLOTS // 16)
    image_keys = jax.random.split(jax.random.fold_in(key, 12), IMAGES)
    ranks = jax.vmap(lambda single: jax.random.permutation(single, SLOTS))(image_keys).astype(jnp.int32)
    padded = (jnp.arange(SLOTS, dtype=jnp.int32)[None, :] >= lengths[:, None]).astype(jnp.int32)
    scores = ranks + SLOTS * padded
    order = jnp.argsort(scores, axis=1, stable=True).astype(jnp.int32)
    return (buckets, order[:, :KEEP])


def draw_bucket_ids(key, part):
    return routing_tables(key)[0]


def draw_keep_order(key, part):
    return routing_tables(key)[1]


def draw_group_counts(key, part):
    most = IMG_MB * MICRO
    groups = IMAGES // most
    least = max(1, most // 4)
    counts = jax.random.randint(jax.random.fold_in(key, 21), (groups,), least, most + 1)
    full_at = jax.random.randint(jax.random.fold_in(key, 22), (), 0, groups)
    return jnp.where(jnp.arange(groups) == full_at, most, counts).astype(jnp.int32)


def block_levels(key, extent, cuts, low, top_value):
    loudness = 1.0
    for axis_at, shards_of in cuts:
        steps = jax.random.uniform(jax.random.fold_in(jax.random.fold_in(key, 6), axis_at), (shards_of,), jnp.float32, low / len(cuts), top_value / len(cuts))
        loudness = loudness * jnp.repeat(jnp.exp(steps), extent[axis_at] // shards_of).reshape((-1,) + (1,) * (len(extent) - 1 - axis_at))
    return loudness


def normal_values(own_key, shape, deviation, bound, cuts=(), held_as=jnp.bfloat16):
    gain = block_levels(own_key, shape, cuts, -0.22, 0.18) if cuts else 1.0
    entries = jax.random.normal(own_key, shape, jnp.float32) * deviation * gain
    return jnp.minimum(jnp.maximum(entries, -bound), bound).astype(held_as)


def setup_inputs(seed: int = 0) -> dict:
    splits = jax.random.split(jax.random.key(seed), 17)
    tokens = normal_values(splits[0], (IMAGES, SLOTS, D), 1.0, 6.0, ((0, 16),))
    conditioning = normal_values(splits[1], (IMAGES, D), 1.0, 6.0, ((0, 16),))
    bucket_ids = draw_bucket_ids(jax.random.fold_in(splits[16], 71), 0)
    keep_order = draw_keep_order(jax.random.fold_in(splits[16], 71), 0)
    group_counts = draw_group_counts(jax.random.fold_in(splits[16], 71), 0)
    cotangent = normal_values(splits[5], (IMAGES, SLOTS, D), 1.0, 6.0, ((0, 16),))
    modulation_weight = normal_values(splits[6], (D, 6 * D), D ** -0.5, 0.1875, ((0, 16),))
    modulation_bias = normal_values(splits[7], (6 * D,), 0.5, 3.0)
    input_weight = normal_values(splits[8], (3, D, D), D ** -0.5, 0.1875, ((1, 16), (2, 2)))
    query_value_bias = normal_values(splits[9], (2, D), 0.5, 3.0, ((1, 2),))
    output_weight = normal_values(splits[10], (D, D), (D // 16) ** -0.5, 0.75, ((0, 2), (1, 16)))
    output_bias = normal_values(splits[11], (D,), 0.3, 2.0)
    expand_weight = normal_values(splits[12], (D, FF), D ** -0.5, 0.1875, ((0, 16), (1, 2)))
    expand_bias = normal_values(splits[13], (FF,), 0.5, 3.0, ((0, 2),))
    shrink_weight = normal_values(splits[14], (FF, D), FF ** -0.5, 0.09375, ((0, 2), (1, 16)))
    shrink_bias = normal_values(splits[15], (D,), 0.3, 2.0)
    return dict(tokens=tokens, conditioning=conditioning, bucket_ids=bucket_ids, keep_order=keep_order, group_counts=group_counts, cotangent=cotangent, modulation_weight=modulation_weight, modulation_bias=modulation_bias, input_weight=input_weight, query_value_bias=query_value_bias, output_weight=output_weight, output_bias=output_bias, expand_weight=expand_weight, expand_bias=expand_bias, shrink_weight=shrink_weight, shrink_bias=shrink_bias)


@jax.custom_vjp
def low(v):
    return lax.optimization_barrier(v.astype(jnp.bfloat16)).astype(jnp.float32)

@jax.custom_vjp
def low_back(v):
    return v

def low_keep(v):
    return (low(v), None)

def low_pass(kept, grad):
    return (grad,)

def back_keep(v):
    return (v, None)

def back_low(kept, grad):
    return (low(grad),)
low.defvjp(low_keep, low_pass)
low_back.defvjp(back_keep, back_low)
EPSILON = 1e-06
HIGHEST = lax.Precision.HIGHEST

def normalize(rows):
    center = rows - lax.optimization_barrier(jnp.mean(rows, axis=-1, keepdims=True))
    spread = lax.optimization_barrier(jnp.mean(center * center, axis=-1, keepdims=True))
    return center * lax.rsqrt(spread + EPSILON)

def project(rows, matrix):
    return jnp.einsum('gkd,de->gke', rows, matrix, precision=HIGHEST)

def block(tokens_group, cond_group, order_group, valid_group, mod_w, mod_b, incoming_weight, qv_b, outgoing_weight, out_b, expert_weight_rows, exp_b, narrowing_weight, shr_b):
    count = tokens_group.shape[0]
    width = tokens_group.shape[2]
    keep = order_group.shape[1]
    hidden_in = jnp.take_along_axis(tokens_group, order_group[:, :, None], axis=1)
    silu_cond = low(jax.nn.silu(cond_group))
    modulation = low_back(jnp.dot(silu_cond, mod_w, precision=HIGHEST)) + mod_b
    pieces = modulation.reshape(count, 6, 1, width)
    shift_one, scale_one, gate_one = (pieces[:, 0], pieces[:, 1], pieces[:, 2])
    shift_two, scale_two, gate_two = (pieces[:, 3], pieces[:, 4], pieces[:, 5])
    first = low(normalize(hidden_in) * (1.0 + scale_one) + shift_one)
    query = low(low_back(project(first, incoming_weight[0])) + qv_b[0]).reshape(count, keep, HEADS, HEAD_DIM)
    key_rows = low(low_back(project(first, incoming_weight[1]))).reshape(count, keep, HEADS, HEAD_DIM)
    value = low(low_back(project(first, incoming_weight[2])) + qv_b[1]).reshape(count, keep, HEADS, HEAD_DIM)
    keymask = jnp.arange(keep)[None, :] < valid_group[:, None]
    scores = jnp.einsum('gqhd,gkhd->ghqk', query, key_rows, precision=HIGHEST) * HEAD_DIM ** (-0.5)
    scores = low_back(jnp.where(keymask[:, None, None, :], scores, -1e+30))
    expo = jnp.exp(scores - lax.optimization_barrier(jnp.max(scores, axis=-1, keepdims=True)))
    probs = low(expo / lax.optimization_barrier(jnp.sum(expo, axis=-1, keepdims=True)))
    attention_result = low(low_back(jnp.einsum('ghqk,gkhd->gqhd', probs, value, precision=HIGHEST))).reshape(count, keep, width)
    attn_out = low_back(project(attention_result, outgoing_weight)) + out_b
    middle = hidden_in + gate_one * attn_out
    second = low(normalize(middle) * (1.0 + scale_two) + shift_two)
    preactivation_rows = low_back(project(second, expert_weight_rows)) + exp_b
    activated = low(jax.nn.gelu(preactivation_rows, approximate=True))
    mlp_out = low_back(project(activated, narrowing_weight)) + shr_b
    routed_out = jnp.where(keymask[:, :, None], middle + gate_two * mlp_out, hidden_in)
    image_rows = jnp.arange(count)[:, None]
    return tokens_group.at[image_rows, order_group].set(routed_out)

def reference(tokens, conditioning, bucket_ids, keep_order, group_counts, cotangent, modulation_weight, modulation_bias, input_weight, query_value_bias, output_weight, output_bias, expand_weight, expand_bias, shrink_weight, shrink_bias):
    per_group = IMG_MB * MICRO
    groups = IMAGES // per_group
    params = (modulation_weight, modulation_bias, input_weight, query_value_bias, output_weight, output_bias, expand_weight, expand_bias, shrink_weight, shrink_bias)
    params = tuple((weight.astype(jnp.float32) for weight in params))
    lengths = jnp.where(bucket_ids == 0, SLOTS, SLOTS - SLOTS // 16) // 2
    live = jnp.arange(per_group)[None, :] < group_counts[:, None]
    valid = jnp.where(live.reshape(-1), lengths, 0).astype(jnp.int32)

    def shaped(array):
        return array.reshape((groups, per_group) + array.shape[1:])

    def one_group(carry, items):
        tokens_group, cond_group, order_group, valid_group, grad_group = items

        def forward(rows, *weights):
            return block(rows, cond_group.astype(jnp.float32), order_group, valid_group, *weights)
        output, pull = jax.vjp(forward, tokens_group.astype(jnp.float32), *params)
        grads = pull(grad_group.astype(jnp.float32))
        summed = tuple((total + term for total, term in zip(carry, grads[1:])))
        return (summed, (output.astype(jnp.bfloat16), grads[0].astype(jnp.bfloat16)))
    zeros = tuple((jnp.zeros_like(weight) for weight in params))
    sums, (outputs, grads) = lax.scan(one_group, zeros, (shaped(tokens), shaped(conditioning), shaped(keep_order), shaped(valid), shaped(cotangent)))
    return (outputs.reshape(tokens.shape), grads.reshape(tokens.shape), sums[0], sums[1], sums[2], sums[3], sums[4], sums[5], sums[6], sums[7], sums[8], sums[9])
```

```python
import jax
import jax.numpy as jnp
from jax import lax
from jax.sharding import PartitionSpec as P

HEAD_DIM = 72
EPSILON = 1e-06


def normalize(rows):
    center = rows - jnp.mean(rows, axis=-1, keepdims=True)
    spread = jnp.mean(center * center, axis=-1, keepdims=True)
    return center * lax.rsqrt(spread + EPSILON)


def modulated(rows, shift, scale):
    return normalize(rows) * (1.0 + scale) + shift


def gelu_tanh(values):
    return jax.nn.gelu(values, approximate=True)


def model_sum(partial):
    other = lax.ppermute(partial, "mp", [(0, 1), (1, 0)])
    return partial + other


def attention_scores(query, key_rows, keymask, scale_factor):
    scores = (
        jnp.einsum("bqhd,bkhd->bhqk", query, key_rows, preferred_element_type=jnp.float32)
        * scale_factor
    )
    return jnp.where(keymask[:, None, None, :], scores, -1e30)


def body(
    tokens,
    conditioning,
    bucket_ids,
    keep_order,
    group_counts,
    cotangent,
    modulation_weight,
    modulation_bias,
    input_weight,
    query_value_bias,
    output_weight,
    output_bias,
    expand_weight,
    expand_bias,
    shrink_weight,
    shrink_bias,
):
    f32 = jnp.float32
    bf16 = jnp.bfloat16
    batch, slots, width = tokens.shape
    keep = keep_order.shape[1]
    d_shard = modulation_weight.shape[0]
    dp_index = lax.axis_index("dp")
    scale_factor = HEAD_DIM ** (-0.5)

    lengths = jnp.where(bucket_ids == 0, slots, slots - slots // 16) // 2
    valid = jnp.where(jnp.arange(batch) < group_counts[0], lengths, 0).astype(jnp.int32)
    keymask = jnp.arange(keep)[None, :] < valid[:, None]
    rowmask = keymask[:, :, None]

    incoming_weight = lax.all_gather(input_weight, "dp", axis=1, tiled=True)
    outgoing_weight = lax.all_gather(output_weight, "dp", axis=1, tiled=True)
    expert_weight_rows = lax.all_gather(expand_weight, "dp", axis=0, tiled=True)
    narrowing_weight = lax.all_gather(shrink_weight, "dp", axis=1, tiled=True)
    inner = incoming_weight.shape[2]
    heads_here = inner // HEAD_DIM
    qv_bias = query_value_bias.astype(f32)
    outgoing_bias = output_bias.astype(f32)
    expert_bias_rows = expand_bias.astype(f32)
    narrowing_bias = shrink_bias.astype(f32)

    silu_cond = jax.nn.silu(conditioning.astype(f32)).astype(bf16)
    silu_all = lax.all_gather(silu_cond, "dp", axis=0, tiled=True)
    silu_cols = lax.dynamic_slice_in_dim(silu_all, dp_index * d_shard, d_shard, axis=1)
    mod_partial = jnp.dot(silu_cols, modulation_weight, preferred_element_type=f32)
    modulation = lax.psum_scatter(mod_partial, "dp", scatter_dimension=0, tiled=True)
    modulation = modulation + modulation_bias.astype(f32)
    pieces = modulation.reshape(batch, 6, 1, width)
    shift_one, scale_one, gate_one = (pieces[:, 0], pieces[:, 1], pieces[:, 2])
    shift_two, scale_two, gate_two = (pieces[:, 3], pieces[:, 4], pieces[:, 5])

    onehot = (keep_order[:, :, None] == jnp.arange(slots)[None, None, :]).astype(bf16)
    slot_taken = jnp.sum(onehot.astype(f32), axis=1) > 0.5
    hidden_in = jnp.einsum("brs,bsd->brd", onehot, tokens, preferred_element_type=f32)
    grad_rows = jnp.einsum("brs,bsd->brd", onehot, cotangent, preferred_element_type=f32)

    first, pull_first = jax.vjp(modulated, hidden_in, shift_one, scale_one)
    first_reduced = first.astype(bf16)
    projected_rows = jnp.einsum(
        "mzu,lug->lmzg", first_reduced, incoming_weight, preferred_element_type=f32
    )
    query = (projected_rows[0] + qv_bias[0]).astype(bf16).reshape(batch, keep, heads_here, HEAD_DIM)
    key_rows = projected_rows[1].astype(bf16).reshape(batch, keep, heads_here, HEAD_DIM)
    value = (projected_rows[2] + qv_bias[1]).astype(bf16).reshape(batch, keep, heads_here, HEAD_DIM)
    scores = attention_scores(query, key_rows, keymask, scale_factor)
    top = jnp.max(scores, axis=-1, keepdims=True)
    expo = jnp.exp(scores - top)
    total = jnp.sum(expo, axis=-1, keepdims=True)
    probs = expo / total
    log_total = top + jnp.log(total)
    attention_result = (
        jnp.einsum("bhqk,bkhd->bqhd", probs.astype(bf16), value, preferred_element_type=f32)
        .astype(bf16)
        .reshape(batch, keep, inner)
    )
    attn_out = (
        model_sum(
            jnp.einsum("hfc,cj->hfj", attention_result, outgoing_weight, preferred_element_type=f32)
        )
        + outgoing_bias
    )
    middle = hidden_in + gate_one * attn_out
    second, pull_second = jax.vjp(modulated, middle, shift_two, scale_two)
    second_reduced = second.astype(bf16)
    preactivation_rows = (
        jnp.einsum("get,tm->gem", second_reduced, expert_weight_rows, preferred_element_type=f32)
        + expert_bias_rows
    )
    activated, pull_act = jax.vjp(gelu_tanh, preactivation_rows)
    activation_reduced = activated.astype(bf16)
    mlp_out = (
        model_sum(
            jnp.einsum("xwl,lc->xwc", activation_reduced, narrowing_weight, preferred_element_type=f32)
        )
        + narrowing_bias
    )
    routed_out = jnp.where(rowmask, middle + gate_two * mlp_out, hidden_in)
    placed = jnp.einsum("brs,brd->bsd", onehot, routed_out.astype(bf16), preferred_element_type=f32)
    block_out = jnp.where(slot_taken[:, :, None], placed.astype(bf16), tokens)

    grad_final = jnp.where(rowmask, grad_rows, 0.0)
    grad_skip = grad_rows - grad_final
    grad_gate_two = jnp.sum(mlp_out * grad_final, axis=1, keepdims=True)
    grad_mlp = gate_two * grad_final
    perceptron_gradient_reduced = grad_mlp.astype(bf16)
    narrowing_term = jnp.einsum(
        "ehm,eht->mt", activation_reduced, perceptron_gradient_reduced, preferred_element_type=f32
    )
    (grad_pre,) = pull_act(
        jnp.einsum(
            "awm,hm->awh", perceptron_gradient_reduced, narrowing_weight, preferred_element_type=f32
        )
    )
    preactivation_gradient_reduced = grad_pre.astype(bf16)
    widening_term = jnp.einsum(
        "cnq,cne->qe", second_reduced, preactivation_gradient_reduced, preferred_element_type=f32
    )
    grad_second = model_sum(
        jnp.einsum(
            "pem,sm->pes", preactivation_gradient_reduced, expert_weight_rows, preferred_element_type=f32
        )
    )
    grad_middle, grad_shift_two, grad_scale_two = pull_second(grad_second)
    grad_middle = grad_middle + grad_final
    grad_gate_one = jnp.sum(attn_out * grad_middle, axis=1, keepdims=True)
    grad_attn = gate_one * grad_middle
    attention_gradient_reduced = grad_attn.astype(bf16)
    output_summand = jnp.einsum(
        "tyo,tyq->oq", attention_result, attention_gradient_reduced, preferred_element_type=f32
    )
    grad_attended = (
        jnp.einsum("znx,ox->zno", attention_gradient_reduced, outgoing_weight, preferred_element_type=f32)
        .astype(bf16)
        .reshape(batch, keep, heads_here, HEAD_DIM)
    )
    again = attention_scores(query, key_rows, keymask, scale_factor)
    probs_again = jnp.exp(again - log_total)
    grad_probs = jnp.einsum("bqhd,bkhd->bhqk", grad_attended, value, preferred_element_type=f32)
    grad_value = jnp.einsum(
        "bhqk,bqhd->bkhd", probs_again.astype(bf16), grad_attended, preferred_element_type=f32
    )
    inner_sum = jnp.sum(probs_again * grad_probs, axis=-1, keepdims=True)
    grad_scores = (probs_again * (grad_probs - inner_sum)).astype(bf16)
    grad_query = (
        jnp.einsum("bhqk,bkhd->bqhd", grad_scores, key_rows, preferred_element_type=f32) * scale_factor
    )
    grad_key = (
        jnp.einsum("bhqk,bqhd->bkhd", grad_scores, query, preferred_element_type=f32) * scale_factor
    )
    grad_proj = jnp.stack([grad_query, grad_key, grad_value]).reshape(3, batch, keep, inner)
    query_value_term = jnp.sum(grad_proj[::2], axis=(1, 2))
    projection_gradient_reduced = grad_proj.astype(bf16)
    input_summand = jnp.einsum(
        "iyj,fiyu->jfu", first_reduced, projection_gradient_reduced, preferred_element_type=f32
    )
    grad_first = model_sum(
        jnp.einsum(
            "pniu,psu->nis", projection_gradient_reduced, incoming_weight, preferred_element_type=f32
        )
    )
    grad_hidden, grad_shift_one, grad_scale_one = pull_first(grad_first)
    grad_total = grad_hidden + grad_middle + grad_skip
    placed_grad = jnp.einsum(
        "brs,brd->bsd", onehot, grad_total.astype(bf16), preferred_element_type=f32
    )
    tokens_grad = jnp.where(slot_taken[:, :, None], placed_grad.astype(bf16), cotangent)

    grad_mod = jnp.concatenate(
        [grad_shift_one, grad_scale_one, grad_gate_one, grad_shift_two, grad_scale_two, grad_gate_two],
        axis=1,
    ).reshape(batch, 6 * width)
    grad_mod_all = lax.all_gather(grad_mod.astype(bf16), "dp", axis=0, tiled=True)
    modulation_weight_grad = jnp.einsum(
        "bd,be->de", silu_cols, grad_mod_all, preferred_element_type=f32
    )

    input_weight_grad = jnp.transpose(
        lax.psum_scatter(input_summand, "dp", scatter_dimension=0, tiled=True), (1, 0, 2)
    )
    output_weight_grad = lax.psum_scatter(output_summand, "dp", scatter_dimension=1, tiled=True)
    expand_weight_grad = lax.psum_scatter(widening_term, "dp", scatter_dimension=0, tiled=True)
    shrink_weight_grad = lax.psum_scatter(narrowing_term, "dp", scatter_dimension=1, tiled=True)

    bias_sums = lax.psum(
        (
            jnp.sum(grad_mod, axis=0),
            query_value_term,
            jnp.sum(grad_attn, axis=(0, 1)),
            jnp.sum(grad_pre, axis=(0, 1)),
            jnp.sum(grad_mlp, axis=(0, 1)),
        ),
        "dp",
    )
    return (
        block_out,
        tokens_grad,
        modulation_weight_grad,
        bias_sums[0],
        input_weight_grad,
        bias_sums[1],
        output_weight_grad,
        bias_sums[2],
        expand_weight_grad,
        bias_sums[3],
        shrink_weight_grad,
        bias_sums[4],
    )


def solution(mesh):
    in_specs = (
        P("dp", None, None),
        P("dp", None),
        P("dp"),
        P("dp", None),
        P("dp"),
        P("dp", None, None),
        P("dp", None),
        P(),
        P(None, "dp", "mp"),
        P(None, "mp"),
        P("mp", "dp"),
        P(),
        P("dp", "mp"),
        P("mp"),
        P("mp", "dp"),
        P(),
    )
    out_specs = (
        P("dp", None, None),
        P("dp", None, None),
        P("dp", None),
        P(),
        P(None, "dp", "mp"),
        P(None, "mp"),
        P("mp", "dp"),
        P(),
        P("dp", "mp"),
        P("mp"),
        P("mp", "dp"),
        P(),
    )
    return jax.shard_map(body, mesh=mesh, in_specs=in_specs, out_specs=out_specs, check_vma=False)
```

```python
import functools

import jax
import jax.numpy as jnp
from jax import lax
from jax.sharding import PartitionSpec as P

HEAD_DIM = 72
EPSILON = 1e-06


def normalize(rows):
    center = rows - jnp.mean(rows, axis=-1, keepdims=True)
    spread = jnp.mean(center * center, axis=-1, keepdims=True)
    return center * lax.rsqrt(spread + EPSILON)


def modulated(rows, shift, scale):
    return normalize(rows) * (1.0 + scale) + shift


def gelu_tanh(values):
    return jax.nn.gelu(values, approximate=True)


def model_sum(partial):
    other = lax.ppermute(partial, "mp", [(0, 1), (1, 0)])
    return partial + other


def chip_ring(mesh):
    devices = mesh.devices
    chips = devices.shape[0] // 2
    try:
        coords = [tuple(devices[2 * k, 0].coords) for k in range(chips)]
    except (AttributeError, TypeError):
        return None
    varying = [a for a in range(len(coords[0])) if len({c[a] for c in coords}) > 1]
    if len(varying) != 2 or chips < 4 or chips > 8:
        return None
    sizes = [len({c[a] for c in coords}) for a in varying]
    if 2 not in sizes:
        return None
    short, long = (varying[0], varying[1]) if sizes[0] == 2 else (varying[1], varying[0])
    low_short = min(c[short] for c in coords)
    up = sorted((k for k in range(chips) if coords[k][short] == low_short), key=lambda k: coords[k][long])
    down = sorted((k for k in range(chips) if coords[k][short] != low_short), key=lambda k: -coords[k][long])
    return up + down


class Ring:
    def __init__(self, order):
        self.native = order is None
        if self.native:
            return
        self.order = order
        self.n = len(order)
        position = [0] * self.n
        for p, k in enumerate(order):
            position[k] = p
        self.position = position

        def step(direction):
            pairs = []
            for p, k in enumerate(order):
                nxt = order[(p + direction) % self.n]
                for c in range(2):
                    pairs.append((2 * k + c, 2 * nxt + c))
            return pairs

        self.forward = step(1)
        self.backward = step(-1)
        self.swap = [(2 * k + c, 2 * k + 1 - c) for k in range(self.n) for c in range(2)]

    def place(self):
        index = lax.axis_index("dp")
        chip = index // 2
        core = index % 2
        p = jnp.asarray(self.position, jnp.int32)[chip]
        return chip, core, p

    def gather(self, shard, split_axis):
        if self.native:
            return lax.all_gather(shard, "dp", axis=0, tiled=False)
        n = self.n
        chip, core, p = self.place()
        a, b = jnp.split(shard, 2, axis=split_axis)
        got_a, got_b = [a], [b]
        for _ in range(1, n):
            a = lax.ppermute(a, "dp", self.forward)
            b = lax.ppermute(b, "dp", self.backward)
            got_a.append(a)
            got_b.append(b)
        positions = jnp.asarray(self.position, jnp.int32)
        from_a = jnp.take(jnp.stack(got_a), (p - positions) % n, axis=0)
        from_b = jnp.take(jnp.stack(got_b), (positions - p) % n, axis=0)
        mine = jnp.concatenate([from_a, from_b], axis=split_axis + 1)
        other = lax.ppermute(mine, "dp", self.swap)
        pair = jnp.stack([mine, other], axis=1)
        pair = jnp.take(pair, jnp.stack([core, 1 - core]), axis=1)
        return pair.reshape((2 * n,) + shard.shape)

    def reduce(self, blocks, split_axis, wire):
        if self.native:
            return lax.psum_scatter(blocks, "dp", scatter_dimension=0, tiled=False)
        n = self.n
        chip, core, p = self.place()
        order = jnp.asarray(self.order, jnp.int32)
        paired = blocks.reshape((n, 2) + blocks.shape[1:])
        mine = jnp.take(paired, core, axis=1)
        theirs = jnp.take(paired, 1 - core, axis=1)
        summed = mine + lax.ppermute(theirs, "dp", self.swap)
        half_a, half_b = jnp.split(summed, 2, axis=split_axis + 1)
        results = []
        for half, perm, sign in ((half_a, self.forward, 1), (half_b, self.backward, -1)):
            carried = None
            for t in range(1, n):
                own = lax.dynamic_index_in_dim(half, order[(p - sign * t) % n], axis=0, keepdims=False)
                total = own if carried is None else carried + own
                carried = lax.ppermute(total.astype(wire), "dp", perm).astype(jnp.float32)
            own = lax.dynamic_index_in_dim(half, chip, axis=0, keepdims=False)
            results.append(carried + own)
        return jnp.concatenate(results, axis=split_axis)


def attention_scores(query, key_rows, keymask, scale_factor):
    scores = (
        jnp.einsum("bqhd,bkhd->bhqk", query, key_rows, preferred_element_type=jnp.float32)
        * scale_factor
    )
    return jnp.where(keymask[:, None, None, :], scores, -1e30)


def body(
    ring,
    tokens,
    conditioning,
    bucket_ids,
    keep_order,
    group_counts,
    cotangent,
    modulation_weight,
    modulation_bias,
    input_weight,
    query_value_bias,
    output_weight,
    output_bias,
    expand_weight,
    expand_bias,
    shrink_weight,
    shrink_bias,
):
    f32 = jnp.float32
    bf16 = jnp.bfloat16
    batch, slots, width = tokens.shape
    keep = keep_order.shape[1]
    d_shard = modulation_weight.shape[0]
    n_dp = width // d_shard
    dp_index = lax.axis_index("dp")
    scale_factor = HEAD_DIM ** (-0.5)

    lengths = jnp.where(bucket_ids == 0, slots, slots - slots // 16) // 2
    valid = jnp.where(jnp.arange(batch) < group_counts[0], lengths, 0).astype(jnp.int32)
    keymask = jnp.arange(keep)[None, :] < valid[:, None]
    rowmask = keymask[:, :, None]

    incoming_weight = ring.gather(input_weight, 2)
    outgoing_weight = ring.gather(output_weight, 0)
    expert_weight_rows = ring.gather(expand_weight, 1).reshape(width, -1)
    narrowing_weight = ring.gather(shrink_weight, 0)
    inner = incoming_weight.shape[3]
    heads_here = inner // HEAD_DIM
    qv_bias = query_value_bias.astype(f32)
    outgoing_bias = output_bias.astype(f32)
    expert_bias_rows = expand_bias.astype(f32)
    narrowing_bias = shrink_bias.astype(f32)

    silu_cond = jax.nn.silu(conditioning.astype(f32)).astype(bf16)
    silu_all = ring.gather(silu_cond, 1).reshape(-1, width)
    silu_cols = lax.dynamic_slice_in_dim(silu_all, dp_index * d_shard, d_shard, axis=1)
    mod_partial = jnp.dot(silu_cols, modulation_weight, preferred_element_type=f32)
    modulation = ring.reduce(mod_partial.reshape(n_dp, batch, -1), 1, f32)
    modulation = modulation + modulation_bias.astype(f32)
    pieces = modulation.reshape(batch, 6, 1, width)
    shift_one, scale_one, gate_one = (pieces[:, 0], pieces[:, 1], pieces[:, 2])
    shift_two, scale_two, gate_two = (pieces[:, 3], pieces[:, 4], pieces[:, 5])

    onehot = (keep_order[:, :, None] == jnp.arange(slots)[None, None, :]).astype(bf16)
    slot_taken = jnp.sum(onehot.astype(f32), axis=1) > 0.5
    hidden_in = jnp.einsum("brs,bsd->brd", onehot, tokens, preferred_element_type=f32)
    grad_rows = jnp.einsum("brs,bsd->brd", onehot, cotangent, preferred_element_type=f32)

    def blocks(rows):
        return rows.reshape(batch, keep, n_dp, d_shard)

    first, pull_first = jax.vjp(modulated, hidden_in, shift_one, scale_one)
    first_reduced = first.astype(bf16)
    projected_rows = jnp.einsum(
        "bkdr,dlru->lbku", blocks(first_reduced), incoming_weight, preferred_element_type=f32
    )
    query = (projected_rows[0] + qv_bias[0]).astype(bf16).reshape(batch, keep, heads_here, HEAD_DIM)
    key_rows = projected_rows[1].astype(bf16).reshape(batch, keep, heads_here, HEAD_DIM)
    value = (projected_rows[2] + qv_bias[1]).astype(bf16).reshape(batch, keep, heads_here, HEAD_DIM)
    scores = attention_scores(query, key_rows, keymask, scale_factor)
    top = jnp.max(scores, axis=-1, keepdims=True)
    expo = jnp.exp(scores - top)
    total = jnp.sum(expo, axis=-1, keepdims=True)
    probs = expo / total
    log_total = top + jnp.log(total)
    attention_result = (
        jnp.einsum("bhqk,bkhd->bqhd", probs.astype(bf16), value, preferred_element_type=f32)
        .astype(bf16)
        .reshape(batch, keep, inner)
    )
    attn_out = (
        model_sum(
            jnp.einsum(
                "bkh,dhr->bkdr", attention_result, outgoing_weight, preferred_element_type=f32
            ).reshape(batch, keep, width)
        )
        + outgoing_bias
    )
    middle = hidden_in + gate_one * attn_out
    second, pull_second = jax.vjp(modulated, middle, shift_two, scale_two)
    second_reduced = second.astype(bf16)
    preactivation_rows = (
        jnp.einsum("get,tm->gem", second_reduced, expert_weight_rows, preferred_element_type=f32)
        + expert_bias_rows
    )
    activated, pull_act = jax.vjp(gelu_tanh, preactivation_rows)
    activation_reduced = activated.astype(bf16)
    mlp_out = (
        model_sum(
            jnp.einsum(
                "bku,dur->bkdr", activation_reduced, narrowing_weight, preferred_element_type=f32
            ).reshape(batch, keep, width)
        )
        + narrowing_bias
    )
    routed_out = jnp.where(rowmask, middle + gate_two * mlp_out, hidden_in)
    placed = jnp.einsum("brs,brd->bsd", onehot, routed_out.astype(bf16), preferred_element_type=f32)
    block_out = jnp.where(slot_taken[:, :, None], placed.astype(bf16), tokens)

    grad_final = jnp.where(rowmask, grad_rows, 0.0)
    grad_skip = grad_rows - grad_final
    grad_gate_two = jnp.sum(mlp_out * grad_final, axis=1, keepdims=True)
    grad_mlp = gate_two * grad_final
    perceptron_gradient_reduced = grad_mlp.astype(bf16)
    narrowing_term = jnp.einsum(
        "bku,bkdr->dur", activation_reduced, blocks(perceptron_gradient_reduced), preferred_element_type=f32
    )
    shrink_weight_grad = ring.reduce(narrowing_term, 0, bf16)
    (grad_pre,) = pull_act(
        jnp.einsum(
            "bkdr,dur->bku", blocks(perceptron_gradient_reduced), narrowing_weight, preferred_element_type=f32
        )
    )
    preactivation_gradient_reduced = grad_pre.astype(bf16)
    widening_term = jnp.einsum(
        "cnq,cne->qe", second_reduced, preactivation_gradient_reduced, preferred_element_type=f32
    )
    expand_weight_grad = ring.reduce(widening_term.reshape(n_dp, d_shard, -1), 1, bf16)
    grad_second = model_sum(
        jnp.einsum(
            "pem,sm->pes", preactivation_gradient_reduced, expert_weight_rows, preferred_element_type=f32
        )
    )
    grad_middle, grad_shift_two, grad_scale_two = pull_second(grad_second)
    grad_middle = grad_middle + grad_final
    grad_gate_one = jnp.sum(attn_out * grad_middle, axis=1, keepdims=True)
    grad_attn = gate_one * grad_middle
    attention_gradient_reduced = grad_attn.astype(bf16)
    output_summand = jnp.einsum(
        "bkh,bkdr->dhr", attention_result, blocks(attention_gradient_reduced), preferred_element_type=f32
    )
    output_weight_grad = ring.reduce(output_summand, 0, bf16)
    grad_attended = (
        jnp.einsum(
            "bkdr,dhr->bkh", blocks(attention_gradient_reduced), outgoing_weight, preferred_element_type=f32
        )
        .astype(bf16)
        .reshape(batch, keep, heads_here, HEAD_DIM)
    )
    again = attention_scores(query, key_rows, keymask, scale_factor)
    probs_again = jnp.exp(again - log_total)
    grad_probs = jnp.einsum("bqhd,bkhd->bhqk", grad_attended, value, preferred_element_type=f32)
    grad_value = jnp.einsum(
        "bhqk,bqhd->bkhd", probs_again.astype(bf16), grad_attended, preferred_element_type=f32
    )
    inner_sum = jnp.sum(probs_again * grad_probs, axis=-1, keepdims=True)
    grad_scores = (probs_again * (grad_probs - inner_sum)).astype(bf16)
    grad_query = (
        jnp.einsum("bhqk,bkhd->bqhd", grad_scores, key_rows, preferred_element_type=f32) * scale_factor
    )
    grad_key = (
        jnp.einsum("bhqk,bqhd->bkhd", grad_scores, query, preferred_element_type=f32) * scale_factor
    )
    grad_proj = jnp.stack([grad_query, grad_key, grad_value]).reshape(3, batch, keep, inner)
    query_value_term = jnp.sum(grad_proj[::2], axis=(1, 2))
    projection_gradient_reduced = grad_proj.astype(bf16)
    input_summand = jnp.einsum(
        "bkdr,lbku->dlru", blocks(first_reduced), projection_gradient_reduced, preferred_element_type=f32
    )
    input_weight_grad = ring.reduce(input_summand, 2, bf16)
    grad_first = model_sum(
        jnp.einsum(
            "lbku,dlru->bkdr", projection_gradient_reduced, incoming_weight, preferred_element_type=f32
        ).reshape(batch, keep, width)
    )
    grad_hidden, grad_shift_one, grad_scale_one = pull_first(grad_first)
    grad_total = grad_hidden + grad_middle + grad_skip
    placed_grad = jnp.einsum(
        "brs,brd->bsd", onehot, grad_total.astype(bf16), preferred_element_type=f32
    )
    tokens_grad = jnp.where(slot_taken[:, :, None], placed_grad.astype(bf16), cotangent)

    grad_mod = jnp.concatenate(
        [grad_shift_one, grad_scale_one, grad_gate_one, grad_shift_two, grad_scale_two, grad_gate_two],
        axis=1,
    ).reshape(batch, 6 * width)
    bias_terms = (
        jnp.sum(grad_mod, axis=0),
        query_value_term.reshape(-1),
        jnp.sum(grad_attn, axis=(0, 1)),
        jnp.sum(grad_pre, axis=(0, 1)),
        jnp.sum(grad_mlp, axis=(0, 1)),
    )
    gathered = ring.gather(jnp.concatenate((grad_mod.reshape(-1),) + bias_terms), 0)
    grad_mod_all = gathered[:, : grad_mod.size].reshape(-1, 6 * width).astype(bf16)
    modulation_weight_grad = jnp.einsum(
        "bd,be->de", silu_cols, grad_mod_all, preferred_element_type=f32
    )
    bias_sums = []
    offset = grad_mod.size
    for term in bias_terms:
        bias_sums.append(jnp.sum(gathered[:, offset : offset + term.size], axis=0))
        offset += term.size
    return (
        block_out,
        tokens_grad,
        modulation_weight_grad,
        bias_sums[0],
        input_weight_grad,
        bias_sums[1].reshape(query_value_term.shape),
        output_weight_grad,
        bias_sums[2],
        expand_weight_grad,
        bias_sums[3],
        shrink_weight_grad,
        bias_sums[4],
    )


def solution(mesh):
    in_specs = (
        P("dp", None, None),
        P("dp", None),
        P("dp"),
        P("dp", None),
        P("dp"),
        P("dp", None, None),
        P("dp", None),
        P(),
        P(None, "dp", "mp"),
        P(None, "mp"),
        P("mp", "dp"),
        P(),
        P("dp", "mp"),
        P("mp"),
        P("mp", "dp"),
        P(),
    )
    out_specs = (
        P("dp", None, None),
        P("dp", None, None),
        P("dp", None),
        P(),
        P(None, "dp", "mp"),
        P(None, "mp"),
        P("mp", "dp"),
        P(),
        P("dp", "mp"),
        P("mp"),
        P("mp", "dp"),
        P(),
    )
    return jax.shard_map(functools.partial(body, Ring(chip_ring(mesh))), mesh=mesh, in_specs=in_specs, out_specs=out_specs, check_vma=False)
```

```python
import functools

import jax
import jax.numpy as jnp
from jax import lax
from jax.sharding import PartitionSpec as P

HEAD_DIM = 72
EPSILON = 1e-06


def normalize(rows):
    center = rows - jnp.mean(rows, axis=-1, keepdims=True)
    spread = jnp.mean(center * center, axis=-1, keepdims=True)
    return center * lax.rsqrt(spread + EPSILON)


def modulated(rows, shift, scale):
    return normalize(rows) * (1.0 + scale) + shift


def gelu_tanh(values):
    return jax.nn.gelu(values, approximate=True)


def model_sum(partial):
    other = lax.ppermute(partial, "mp", [(0, 1), (1, 0)])
    return partial + other


def chip_ring(mesh):
    devices = mesh.devices
    chips = devices.shape[0] // 2
    try:
        coords = [tuple(devices[2 * k, 0].coords) for k in range(chips)]
    except (AttributeError, TypeError):
        return None
    varying = [a for a in range(len(coords[0])) if len({c[a] for c in coords}) > 1]
    if len(varying) != 2 or chips < 4 or chips > 8:
        return None
    sizes = [len({c[a] for c in coords}) for a in varying]
    if 2 not in sizes:
        return None
    short, long = (varying[0], varying[1]) if sizes[0] == 2 else (varying[1], varying[0])
    low_short = min(c[short] for c in coords)
    up = sorted((k for k in range(chips) if coords[k][short] == low_short), key=lambda k: coords[k][long])
    down = sorted((k for k in range(chips) if coords[k][short] != low_short), key=lambda k: -coords[k][long])
    return up + down


class Ring:
    def __init__(self, order):
        self.native = order is None
        if self.native:
            return
        self.order = order
        self.n = len(order)
        position = [0] * self.n
        for p, k in enumerate(order):
            position[k] = p
        self.position = position

        def step(direction):
            pairs = []
            for p, k in enumerate(order):
                nxt = order[(p + direction) % self.n]
                for c in range(2):
                    pairs.append((2 * k + c, 2 * nxt + c))
            return pairs

        self.forward = step(1)
        self.backward = step(-1)
        self.swap = [(2 * k + c, 2 * k + 1 - c) for k in range(self.n) for c in range(2)]
        n_dp = 2 * self.n
        self.bits = n_dp.bit_length() - 1 if n_dp & (n_dp - 1) == 0 else None

    def place(self):
        index = lax.axis_index("dp")
        chip = index // 2
        core = index % 2
        p = jnp.asarray(self.position, jnp.int32)[chip]
        return chip, core, p

    def gather(self, shards):
        if self.native:
            return [lax.all_gather(s, "dp", axis=0, tiled=False) for s in shards]
        n = self.n
        chip, core, p = self.place()
        flat = jnp.concatenate([s.reshape(-1) for s in shards])
        a, b = jnp.split(flat, 2)
        got_a, got_b = [a], [b]
        for _ in range(1, n):
            a = lax.ppermute(a, "dp", self.forward)
            b = lax.ppermute(b, "dp", self.backward)
            got_a.append(a)
            got_b.append(b)
        positions = jnp.asarray(self.position, jnp.int32)
        from_a = jnp.take(jnp.stack(got_a), (p - positions) % n, axis=0)
        from_b = jnp.take(jnp.stack(got_b), (positions - p) % n, axis=0)
        mine = jnp.concatenate([from_a, from_b], axis=1)
        other = lax.ppermute(mine, "dp", self.swap)
        pair = jnp.stack([mine, other], axis=1)
        pair = jnp.take(pair, jnp.stack([core, 1 - core]), axis=1).reshape(2 * n, -1)
        out = []
        offset = 0
        for s in shards:
            out.append(pair[:, offset : offset + s.size].reshape((2 * n,) + s.shape))
            offset += s.size
        return out

    def reduce(self, block_sets, wire):
        if self.native:
            return [lax.psum_scatter(b, "dp", scatter_dimension=0, tiled=False) for b in block_sets]
        n = self.n
        chip, core, p = self.place()
        order = jnp.asarray(self.order, jnp.int32)
        mines, theirs = [], []
        for blocks in block_sets:
            paired = blocks.reshape(n, 2, -1)
            mines.append(jnp.take(paired, core, axis=1))
            theirs.append(jnp.take(paired, 1 - core, axis=1))
        summed = jnp.concatenate(mines, axis=1) + lax.ppermute(
            jnp.concatenate(theirs, axis=1), "dp", self.swap
        )
        half_a, half_b = jnp.split(summed, 2, axis=1)
        results = []
        for half, perm, sign in ((half_a, self.forward, 1), (half_b, self.backward, -1)):
            carried = None
            for t in range(1, n):
                own = lax.dynamic_index_in_dim(half, order[(p - sign * t) % n], axis=0, keepdims=False)
                total = own if carried is None else carried + own
                carried = lax.ppermute(total.astype(wire), "dp", perm).astype(jnp.float32)
            own = lax.dynamic_index_in_dim(half, chip, axis=0, keepdims=False)
            results.append(carried + own)
        flat = jnp.concatenate(results)
        out = []
        offset = 0
        for blocks in block_sets:
            size = blocks[0].size
            out.append(flat[offset : offset + size].reshape(blocks.shape[1:]))
            offset += size
        return out

    def small_gather(self, shard):
        if self.native or self.bits is None:
            return lax.all_gather(shard, "dp", axis=0, tiled=False)
        index = lax.axis_index("dp")
        held = shard[None]
        for bit in range(self.bits):
            partner = [(d, d ^ (1 << bit)) for d in range(2 * self.n)]
            other = lax.ppermute(held, "dp", partner)
            low = (index >> bit) % 2 == 0
            held = jnp.where(low, jnp.concatenate([held, other]), jnp.concatenate([other, held]))
        return held

    def small_reduce(self, blocks):
        if self.native or self.bits is None:
            return lax.psum_scatter(blocks, "dp", scatter_dimension=0, tiled=False)
        index = lax.axis_index("dp")
        held = blocks
        for bit in reversed(range(self.bits)):
            partner = [(d, d ^ (1 << bit)) for d in range(2 * self.n)]
            half = held.shape[0] // 2
            low_part, high_part = held[:half], held[half:]
            low = (index >> bit) % 2 == 0
            keep = jnp.where(low, low_part, high_part)
            give = jnp.where(low, high_part, low_part)
            held = keep + lax.ppermute(give, "dp", partner)
        return held[0]


def attention_scores(query, key_rows, keymask, scale_factor):
    scores = (
        jnp.einsum("bqhd,bkhd->bhqk", query, key_rows, preferred_element_type=jnp.float32)
        * scale_factor
    )
    return jnp.where(keymask[:, None, None, :], scores, -1e30)


def body(
    ring,
    tokens,
    conditioning,
    bucket_ids,
    keep_order,
    group_counts,
    cotangent,
    modulation_weight,
    modulation_bias,
    input_weight,
    query_value_bias,
    output_weight,
    output_bias,
    expand_weight,
    expand_bias,
    shrink_weight,
    shrink_bias,
):
    f32 = jnp.float32
    bf16 = jnp.bfloat16
    batch, slots, width = tokens.shape
    keep = keep_order.shape[1]
    d_shard = modulation_weight.shape[0]
    n_dp = width // d_shard
    dp_index = lax.axis_index("dp")
    scale_factor = HEAD_DIM ** (-0.5)

    lengths = jnp.where(bucket_ids == 0, slots, slots - slots // 16) // 2
    valid = jnp.where(jnp.arange(batch) < group_counts[0], lengths, 0).astype(jnp.int32)
    keymask = jnp.arange(keep)[None, :] < valid[:, None]
    rowmask = keymask[:, :, None]

    incoming_weight, outgoing_weight = ring.gather([input_weight, output_weight])
    expert_weight_rows, narrowing_weight = ring.gather([expand_weight, shrink_weight])
    expert_weight_rows = expert_weight_rows.reshape(width, -1)
    inner = incoming_weight.shape[3]
    heads_here = inner // HEAD_DIM
    qv_bias = query_value_bias.astype(f32)
    outgoing_bias = output_bias.astype(f32)
    expert_bias_rows = expand_bias.astype(f32)
    narrowing_bias = shrink_bias.astype(f32)

    silu_cond = jax.nn.silu(conditioning.astype(f32)).astype(bf16)
    silu_all = ring.small_gather(silu_cond).reshape(-1, width)
    silu_cols = lax.dynamic_slice_in_dim(silu_all, dp_index * d_shard, d_shard, axis=1)
    mod_partial = jnp.dot(silu_cols, modulation_weight, preferred_element_type=f32)
    modulation = ring.small_reduce(mod_partial.reshape(n_dp, batch, -1))
    modulation = modulation + modulation_bias.astype(f32)
    pieces = modulation.reshape(batch, 6, 1, width)
    shift_one, scale_one, gate_one = (pieces[:, 0], pieces[:, 1], pieces[:, 2])
    shift_two, scale_two, gate_two = (pieces[:, 3], pieces[:, 4], pieces[:, 5])

    onehot = (keep_order[:, :, None] == jnp.arange(slots)[None, None, :]).astype(bf16)
    slot_taken = jnp.sum(onehot.astype(f32), axis=1) > 0.5
    hidden_in = jnp.einsum("brs,bsd->brd", onehot, tokens, preferred_element_type=f32)
    grad_rows = jnp.einsum("brs,bsd->brd", onehot, cotangent, preferred_element_type=f32)

    def blocks(rows):
        return rows.reshape(batch, keep, n_dp, d_shard)

    first, pull_first = jax.vjp(modulated, hidden_in, shift_one, scale_one)
    first_reduced = first.astype(bf16)
    projected_rows = jnp.einsum(
        "bkdr,dlru->lbku", blocks(first_reduced), incoming_weight, preferred_element_type=f32
    )
    query = (projected_rows[0] + qv_bias[0]).astype(bf16).reshape(batch, keep, heads_here, HEAD_DIM)
    key_rows = projected_rows[1].astype(bf16).reshape(batch, keep, heads_here, HEAD_DIM)
    value = (projected_rows[2] + qv_bias[1]).astype(bf16).reshape(batch, keep, heads_here, HEAD_DIM)
    scores = attention_scores(query, key_rows, keymask, scale_factor)
    top = jnp.max(scores, axis=-1, keepdims=True)
    expo = jnp.exp(scores - top)
    total = jnp.sum(expo, axis=-1, keepdims=True)
    probs = expo / total
    log_total = top + jnp.log(total)
    attention_result = (
        jnp.einsum("bhqk,bkhd->bqhd", probs.astype(bf16), value, preferred_element_type=f32)
        .astype(bf16)
        .reshape(batch, keep, inner)
    )
    attn_out = (
        model_sum(
            jnp.einsum(
                "bkh,dhr->bkdr", attention_result, outgoing_weight, preferred_element_type=f32
            ).reshape(batch, keep, width)
        )
        + outgoing_bias
    )
    middle = hidden_in + gate_one * attn_out
    second, pull_second = jax.vjp(modulated, middle, shift_two, scale_two)
    second_reduced = second.astype(bf16)
    preactivation_rows = (
        jnp.einsum("get,tm->gem", second_reduced, expert_weight_rows, preferred_element_type=f32)
        + expert_bias_rows
    )
    activated, pull_act = jax.vjp(gelu_tanh, preactivation_rows)
    activation_reduced = activated.astype(bf16)
    mlp_out = (
        model_sum(
            jnp.einsum(
                "bku,dur->bkdr", activation_reduced, narrowing_weight, preferred_element_type=f32
            ).reshape(batch, keep, width)
        )
        + narrowing_bias
    )
    routed_out = jnp.where(rowmask, middle + gate_two * mlp_out, hidden_in)
    placed = jnp.einsum("brs,brd->bsd", onehot, routed_out.astype(bf16), preferred_element_type=f32)
    block_out = jnp.where(slot_taken[:, :, None], placed.astype(bf16), tokens)

    grad_final = jnp.where(rowmask, grad_rows, 0.0)
    grad_skip = grad_rows - grad_final
    grad_gate_two = jnp.sum(mlp_out * grad_final, axis=1, keepdims=True)
    grad_mlp = gate_two * grad_final
    perceptron_gradient_reduced = grad_mlp.astype(bf16)
    narrowing_term = jnp.einsum(
        "bku,bkdr->dur", activation_reduced, blocks(perceptron_gradient_reduced), preferred_element_type=f32
    )
    (grad_pre,) = pull_act(
        jnp.einsum(
            "bkdr,dur->bku", blocks(perceptron_gradient_reduced), narrowing_weight, preferred_element_type=f32
        )
    )
    preactivation_gradient_reduced = grad_pre.astype(bf16)
    widening_term = jnp.einsum(
        "cnq,cne->qe", second_reduced, preactivation_gradient_reduced, preferred_element_type=f32
    )
    expand_weight_grad, shrink_weight_grad = ring.reduce(
        [widening_term.reshape(n_dp, d_shard, -1), narrowing_term], bf16
    )
    grad_second = model_sum(
        jnp.einsum(
            "pem,sm->pes", preactivation_gradient_reduced, expert_weight_rows, preferred_element_type=f32
        )
    )
    grad_middle, grad_shift_two, grad_scale_two = pull_second(grad_second)
    grad_middle = grad_middle + grad_final
    grad_gate_one = jnp.sum(attn_out * grad_middle, axis=1, keepdims=True)
    grad_attn = gate_one * grad_middle
    attention_gradient_reduced = grad_attn.astype(bf16)
    output_summand = jnp.einsum(
        "bkh,bkdr->dhr", attention_result, blocks(attention_gradient_reduced), preferred_element_type=f32
    )
    grad_attended = (
        jnp.einsum(
            "bkdr,dhr->bkh", blocks(attention_gradient_reduced), outgoing_weight, preferred_element_type=f32
        )
        .astype(bf16)
        .reshape(batch, keep, heads_here, HEAD_DIM)
    )
    again = attention_scores(query, key_rows, keymask, scale_factor)
    probs_again = jnp.exp(again - log_total)
    grad_probs = jnp.einsum("bqhd,bkhd->bhqk", grad_attended, value, preferred_element_type=f32)
    grad_value = jnp.einsum(
        "bhqk,bqhd->bkhd", probs_again.astype(bf16), grad_attended, preferred_element_type=f32
    )
    inner_sum = jnp.sum(probs_again * grad_probs, axis=-1, keepdims=True)
    grad_scores = (probs_again * (grad_probs - inner_sum)).astype(bf16)
    grad_query = (
        jnp.einsum("bhqk,bkhd->bqhd", grad_scores, key_rows, preferred_element_type=f32) * scale_factor
    )
    grad_key = (
        jnp.einsum("bhqk,bqhd->bkhd", grad_scores, query, preferred_element_type=f32) * scale_factor
    )
    grad_proj = jnp.stack([grad_query, grad_key, grad_value]).reshape(3, batch, keep, inner)
    query_value_term = jnp.sum(grad_proj[::2], axis=(1, 2))
    projection_gradient_reduced = grad_proj.astype(bf16)
    input_summand = jnp.einsum(
        "bkdr,lbku->dlru", blocks(first_reduced), projection_gradient_reduced, preferred_element_type=f32
    )
    input_weight_grad, output_weight_grad = ring.reduce([input_summand, output_summand], bf16)
    grad_first = model_sum(
        jnp.einsum(
            "lbku,dlru->bkdr", projection_gradient_reduced, incoming_weight, preferred_element_type=f32
        ).reshape(batch, keep, width)
    )
    grad_hidden, grad_shift_one, grad_scale_one = pull_first(grad_first)
    grad_total = grad_hidden + grad_middle + grad_skip
    placed_grad = jnp.einsum(
        "brs,brd->bsd", onehot, grad_total.astype(bf16), preferred_element_type=f32
    )
    tokens_grad = jnp.where(slot_taken[:, :, None], placed_grad.astype(bf16), cotangent)

    grad_mod = jnp.concatenate(
        [grad_shift_one, grad_scale_one, grad_gate_one, grad_shift_two, grad_scale_two, grad_gate_two],
        axis=1,
    ).reshape(batch, 6 * width)
    bias_terms = (
        jnp.sum(grad_mod, axis=0),
        query_value_term.reshape(-1),
        jnp.sum(grad_attn, axis=(0, 1)),
        jnp.sum(grad_pre, axis=(0, 1)),
        jnp.sum(grad_mlp, axis=(0, 1)),
    )
    gathered = ring.small_gather(jnp.concatenate((grad_mod.reshape(-1),) + bias_terms))
    grad_mod_all = gathered[:, : grad_mod.size].reshape(-1, 6 * width).astype(bf16)
    modulation_weight_grad = jnp.einsum(
        "bd,be->de", silu_cols, grad_mod_all, preferred_element_type=f32
    )
    bias_sums = []
    offset = grad_mod.size
    for term in bias_terms:
        bias_sums.append(jnp.sum(gathered[:, offset : offset + term.size], axis=0))
        offset += term.size
    return (
        block_out,
        tokens_grad,
        modulation_weight_grad,
        bias_sums[0],
        input_weight_grad,
        bias_sums[1].reshape(query_value_term.shape),
        output_weight_grad,
        bias_sums[2],
        expand_weight_grad,
        bias_sums[3],
        shrink_weight_grad,
        bias_sums[4],
    )


def solution(mesh):
    in_specs = (
        P("dp", None, None),
        P("dp", None),
        P("dp"),
        P("dp", None),
        P("dp"),
        P("dp", None, None),
        P("dp", None),
        P(),
        P(None, "dp", "mp"),
        P(None, "mp"),
        P("mp", "dp"),
        P(),
        P("dp", "mp"),
        P("mp"),
        P("mp", "dp"),
        P(),
    )
    out_specs = (
        P("dp", None, None),
        P("dp", None, None),
        P("dp", None),
        P(),
        P(None, "dp", "mp"),
        P(None, "mp"),
        P("mp", "dp"),
        P(),
        P("dp", "mp"),
        P("mp"),
        P("mp", "dp"),
        P(),
    )
    return jax.shard_map(functools.partial(body, Ring(chip_ring(mesh))), mesh=mesh, in_specs=in_specs, out_specs=out_specs, check_vma=False)
```
